32 devices in a mesh: role: 4 (over z), grp: 4 (over x, core), run: 2 (over y).
Axes of the slice: x: 2, y: 2, z: 4, core: 2. Of those that a mesh axis runs over, the one named last changes fastest.
Arguments:
- prior_fields: float32 [1024, 3, 32, 128], P(('role', 'grp'), None, 'run'), may hold values from -0.4 to 1.4, as said below
- measured_point_location: int32 [512], P('run'), may hold values from 0 to 2047
- measured_depths: float32 [512], P('run'), may hold values from 0.7 to 1.3
- inverse_noise_deviation: float32 [512], P('run'), may hold values from 5 to 40
- sample_noise_draw: float32 [1024, 512], P(None, 'run'), may hold values from -6 to 6
- sample_line_labels: int32 [1024], P(('role', 'grp')), may hold values from 0 to 1023, each once
Outputs:
- analysis: float32 [1024, 3, 32, 128], P(('role', 'grp'), None, 'run')
The draws below stay inside these ranges and needn't reach their ends.
Inputs may be any that keep to these rules, and one draw needn't show every extreme that they name: `prior_fields`: the depth component (index 0 of the second dimension) lies within 0.75 to 1.4, the momenta within -0.4 to 0.4.
All inputs are finite; a program needn't handle non-finite values.
Results may differ from the reference program's by a relative error of at most 0.0003.
Values sent between devices are 32-bit elements; how exact they have to be, the bound alone decides.
A program may use at most 64 MiB of HBM per device.

```python
import math
import jax
import jax.numpy as jnp
from jax import lax

ENSEMBLE_SIZE = 1024
POINTS_ACROSS = 128
RY = 16
OBS_DEV = 256
STEPS = 4
CHEB = 8
LATTICE_LINES = 32
NOBS = 512


def draw_prior_fields(key, part):
    keys = jax.random.split(jax.random.fold_in(key, 7), 2)
    depth = 1.0 + 0.25 * jax.random.uniform(keys[0], (ENSEMBLE_SIZE, 1, LATTICE_LINES, POINTS_ACROSS), jnp.float32, -1.0, 1.0)
    flows = jnp.clip(0.1 * jax.random.normal(keys[1], (ENSEMBLE_SIZE, 2, LATTICE_LINES, POINTS_ACROSS), jnp.float32), -0.4, 0.4)
    return jnp.concatenate([depth, flows], 1).astype(jnp.float32)


def touch_ends(values, key, least, high):
    extent = values.shape
    index_at = [jax.random.randint(jax.random.fold_in(key, axis), (), 0, extent[axis]) for axis in range(len(extent))]
    values = values.at[tuple(index_at)].set(least)
    longest = extent.index(max(extent))
    index_at[longest] = (index_at[longest] + 1) % extent[longest]
    return values.at[tuple(index_at)].set(high)


def shard_levels(rng, dims, cuts, low, high):
    def one(dim, shards_of):
        heights = jax.random.uniform(jax.random.fold_in(jax.random.fold_in(rng, 6), dim), (shards_of,), jnp.float32, low / len(cuts), high / len(cuts))
        return jnp.repeat(jnp.exp(heights), dims[dim] // shards_of).reshape((-1,) + (1,) * (len(dims) - dim - 1))

    factor_of = one(*cuts[0])
    for cut in cuts[1:]:
        factor_of = factor_of * one(*cut)
    return factor_of


def gaussian(own_key, shape, scale, most, cuts=(), kind=jnp.bfloat16):
    entries = jax.random.normal(own_key, shape, jnp.float32) * scale
    if len(cuts) > 0:
        entries = shard_levels(own_key, shape, cuts, -0.22, 0.18) * entries
    return jnp.clip(entries, min=-most, max=most).astype(kind)


def setup_inputs(seed: int = 0) -> dict:
    key_of = jax.random.split(jax.random.key(seed), 7)
    return {
        "prior_fields": draw_prior_fields(jax.random.fold_in(key_of[6], 71), 0),
        "measured_point_location": touch_ends(jax.random.randint(key_of[1], (NOBS,), 0, RY * POINTS_ACROSS), jax.random.fold_in(key_of[1], 1), 0, (RY * POINTS_ACROSS) - 1).astype(jnp.int32),
        "measured_depths": jnp.clip(0.7 + 0.59999996 * jax.random.uniform(key_of[2], (NOBS,), jnp.float32) ** shard_levels(key_of[2], (NOBS,), ((0, 2),), -0.2, 0.2), 0.7, 1.3),
        "inverse_noise_deviation": jnp.clip(jnp.exp(math.log(40.0) - 2.0794415 * jax.random.uniform(key_of[3], (NOBS,), jnp.float32) ** shard_levels(key_of[3], (NOBS,), ((0, 2),), -0.2, 0.2)), 5.0, 40.0),
        "sample_noise_draw": gaussian(key_of[4], (ENSEMBLE_SIZE, NOBS), 1.0, 6.0, ((1, 2),), jnp.float32),
        "sample_line_labels": jax.random.permutation(key_of[5], ENSEMBLE_SIZE).astype(jnp.int32),
    }


gravity = 1.0
courant = 0.35
widen_dispersion = 1.1

def lax_friedrichs(state):
    depth = state[:, 0]
    east = state[:, 1]
    north = state[:, 2]
    press = 0.5 * gravity * depth * depth
    flux_x = jnp.stack([east, east * east / depth + press, east * north / depth], 1)
    flux_y = jnp.stack([north, east * north / depth, north * north / depth + press], 1)
    inner = state[:, :, 1:-1]
    average = 0.25 * (state[:, :, 2:] + state[:, :, :-2] + jnp.roll(inner, 1, 3) + jnp.roll(inner, -1, 3))
    middle = flux_x[:, :, 1:-1]
    return average - 0.5 * courant * (jnp.roll(middle, -1, 3) - jnp.roll(middle, 1, 3)) - 0.5 * courant * (flux_y[:, :, 2:] - flux_y[:, :, :-2])

def prior_strip_slab(strip_slab):
    for step in range(STEPS):
        padded = jnp.concatenate([strip_slab[:, :, -1:], strip_slab, strip_slab[:, :, :1]], 2)
        strip_slab = lax_friedrichs(padded)
    return strip_slab

def reference(prior_fields, measured_point_location, measured_depths, inverse_noise_deviation, sample_noise_draw, sample_line_labels):
    propagated_fields = lax.map(prior_strip_slab, prior_fields.reshape(ENSEMBLE_SIZE // 16, 16, 3, LATTICE_LINES, POINTS_ACROSS)).reshape(ENSEMBLE_SIZE, 3, LATTICE_LINES, POINTS_ACROSS)
    blocks = (jnp.arange(NOBS, dtype=jnp.int32) // OBS_DEV).astype(jnp.int32)
    cells = (blocks * (RY * POINTS_ACROSS) + measured_point_location).astype(jnp.int32)
    depth_flat = propagated_fields[:, 0].reshape(ENSEMBLE_SIZE, LATTICE_LINES * POINTS_ACROSS)
    sampled = inverse_noise_deviation[None, :] * depth_flat[:, cells]
    innovation = inverse_noise_deviation[None, :] * measured_depths[None, :] - sampled + sample_noise_draw[sample_line_labels]
    dispersion_multiplier = math.sqrt(widen_dispersion / (ENSEMBLE_SIZE - 1))
    spread = dispersion_multiplier * (sampled - lax.optimization_barrier(jnp.mean(sampled, axis=0, keepdims=True)))
    gram = jnp.dot(spread, spread.T, precision=lax.Precision.HIGHEST, preferred_element_type=jnp.float32)
    cross = jnp.dot(innovation, spread.T, precision=lax.Precision.HIGHEST, preferred_element_type=jnp.float32)
    upper = 1.0 + jnp.sqrt(jnp.sum(gram * gram))
    theta = (upper + 1.0) / 2.0
    delta = (upper - 1.0) / 2.0
    sigma = theta / delta
    rho = 1.0 / sigma
    residual = cross
    direction = residual / theta
    linear_solution = direction
    for turn in range(CHEB - 1):
        residual = residual - direction - jnp.dot(direction, gram, precision=lax.Precision.HIGHEST, preferred_element_type=jnp.float32)
        rho_next = 1.0 / (2.0 * sigma - rho)
        direction = rho_next * rho * direction + 2.0 * rho_next / delta * residual
        linear_solution = linear_solution + direction
        rho = rho_next
    ensemble_combination = math.sqrt(widen_dispersion) * jnp.eye(ENSEMBLE_SIZE, dtype=jnp.float32) + dispersion_multiplier * linear_solution
    flat = propagated_fields.reshape(ENSEMBLE_SIZE, 3 * LATTICE_LINES * POINTS_ACROSS)
    center = lax.optimization_barrier(jnp.mean(flat, axis=0, keepdims=True))
    result = center + jnp.dot(ensemble_combination, flat - center, precision=lax.Precision.HIGHEST, preferred_element_type=jnp.float32)
    return result.reshape(ENSEMBLE_SIZE, 3, LATTICE_LINES, POINTS_ACROSS)
```

```python
import functools
import math

import jax
import jax.numpy as jnp
from jax import lax
from jax.experimental import pallas as pl
from jax.experimental.pallas import tpu as pltpu
from jax.sharding import PartitionSpec as P

STEPS = 4
CHEB = 8
CHUNKS = 4
TILE = 8

gravity = 1.0
courant = 0.35
widen_dispersion = 1.1

MESH = pl.DeviceIdType.MESH


def advance(fields):
    depth, east, north = fields
    half = 0.5 * courant
    inverse = 1.0 / depth
    press = 0.5 * gravity * depth * depth
    speed_x = east * inverse
    speed_y = north * inverse
    mixed = east * speed_y
    flux_x = (east, east * speed_x + press, mixed)
    flux_y = (north, mixed, north * speed_y + press)
    rows = depth.shape[0]
    out = []
    for q, fx, fy in zip(fields, flux_x, flux_y):
        quarter = 0.25 * q
        mid = quarter[1:-1]
        kx = half * fx[1:-1]
        sides = pltpu.roll(mid - kx, q.shape[2] - 1, 2) + pltpu.roll(mid + kx, 1, 2)
        up = (quarter - half * fy)[2:]
        down = (quarter + half * fy)[: rows - 2]
        out.append(sides + up + down)
    return tuple(out)


def halves(value):
    high = value.astype(jnp.bfloat16)
    return high, (value - high.astype(jnp.float32)).astype(jnp.bfloat16)


def dot(left, right, dims=((1,), (0,))):
    return lax.dot_general(left, right, (dims, ((), ())), preferred_element_type=jnp.float32)


def dot3(left, right, dims=((1,), (0,))):
    (lh, ll), (rh, rl) = left, right
    return dot(lh, rh, dims) + (dot(lh, rl, dims) + dot(ll, rh, dims))


def kernel(
    dims,
    x_ref, loc_ref, inv_ref, noise_ref,
    out_ref,
    halo, stepped, everyone, result, sampled, noise,
    st_hi, st_lo, gram_hi, gram_lo, res, direc, poly,
    halo_send, halo_recv, s_send, s_recv, n_send, n_recv, f_send, f_recv, b_send, b_recv,
):
    nz, nx, nc, ny = dims
    z = lax.axis_index("role")
    grp = lax.axis_index("grp")
    y = lax.axis_index("run")
    x = grp // nc
    c = grp % nc
    rows, _, members, cols = x_ref.shape
    obs = loc_ref.shape[1]
    total = nz * nx * nc * members
    width = halo.shape[1]

    def device(zz, xx, cc, yy):
        return (zz, xx * nc + cc, yy)

    def flat(cc, xx, zz):
        return (cc * nx + xx) * nz + zz

    me = flat(c, x, z)
    offsets = [(dz, dx, dc) for dz in range(nz) for dx in range(nx) for dc in range(nc)][1:]
    far = {0: 0, nz // 2: 2}
    offsets.sort(key=lambda o: (-far.get(o[0], 1), -o[1], -o[2]))

    def shifted(off):
        dz, dx, dc = off
        return lax.rem(z + dz, nz), lax.rem(x + dx, nx), lax.rem(c + dc, nc)

    other_y = lax.rem(y + 1, ny)

    barrier = pltpu.get_barrier_semaphore()
    for off in offsets:
        zz, xx, cc = shifted(off)
        pl.semaphore_signal(barrier, inc=1, device_id=device(zz, xx, cc, y), device_id_type=MESH)
    pl.semaphore_signal(barrier, inc=1, device_id=device(z, x, c, other_y), device_id_type=MESH)
    pl.semaphore_wait(barrier, len(offsets) + 1)

    def remote(src, dst, send, recv, target):
        return pltpu.make_async_remote_copy(
            src_ref=src, dst_ref=dst, send_sem=send, recv_sem=recv, device_id=target, device_id_type=MESH
        )

    per = members // CHUNKS
    halo_copies = []
    for k in range(CHUNKS):
        part = pl.ds(k * per, per)
        pair = (
            remote(x_ref.at[pl.ds(rows - width, width), :, part], halo.at[0, :, :, part],
                   halo_send.at[2 * k], halo_recv.at[2 * k], device(z, x, c, other_y)),
            remote(x_ref.at[pl.ds(0, width), :, part], halo.at[1, :, :, part],
                   halo_send.at[2 * k + 1], halo_recv.at[2 * k + 1], device(z, x, c, other_y)),
        )
        for copy in pair:
            copy.start()
        halo_copies.append(pair)

    def along_z(buf, send, recv):
        return [
            remote(buf.at[c, y, x, z], buf.at[c, y, x, z], send.at[d - 1], recv.at[d - 1],
                   device(lax.rem(z + d, nz), x, c, y))
            for d in range(1, nz)
        ]

    def along_x(buf, send, recv):
        return remote(buf.at[c, y, x], buf.at[c, y, x], send.at[nz], recv.at[nz],
                      device(z, lax.rem(x + 1, nx), c, y))

    def along_y(buf, send, recv):
        return remote(buf.at[c, y], buf.at[c, y], send.at[nz + 1], recv.at[nz + 1],
                      device(z, x, c, other_y))

    def along_core(buf, send, recv):
        return remote(buf.at[c], buf.at[c], send.at[nz + 2], recv.at[nz + 2],
                      device(z, x, lax.rem(c + 1, nc), y))

    noise[c, y, x, z] = noise_ref[...]
    noise_z = along_z(noise, n_send, n_recv)
    for copy in noise_z:
        copy.start()

    for k in range(CHUNKS):
        for copy in halo_copies[k]:
            copy.wait()

        def tile(t, carry):
            at = pl.ds(pl.multiple_of(k * per + t * TILE, TILE), TILE)
            fields = tuple(
                jnp.concatenate([halo[0, :, f, at], x_ref[:, f, at], halo[1, :, f, at]], 0) for f in range(3)
            )
            for step in range(STEPS):
                fields = advance(fields)
            for f in range(3):
                stepped[:, f, at] = fields[f]
            return carry

        lax.fori_loop(0, per // TILE, tile, 0)

    loc = loc_ref[...]
    lanes = lax.broadcasted_iota(jnp.int32, (cols, obs), 0)

    def pick(r, acc):
        hot = jnp.where(loc - r * cols == lanes, 1.0, 0.0).astype(jnp.bfloat16)
        depth = stepped[r, 0]
        d1 = depth.astype(jnp.bfloat16)
        rest = depth - d1.astype(jnp.float32)
        d2 = rest.astype(jnp.bfloat16)
        d3 = (rest - d2.astype(jnp.float32)).astype(jnp.bfloat16)
        return acc + (dot(d1, hot) + (dot(d2, hot) + dot(d3, hot)))

    own_sampled = inv_ref[...] * lax.fori_loop(0, rows, pick, jnp.zeros((members, obs), jnp.float32))
    sampled[c, y, x, z] = own_sampled
    s_z = along_z(sampled, s_send, s_recv)
    for copy in s_z:
        copy.start()

    forward = {}
    for i, off in enumerate(offsets):
        zz, xx, cc = shifted(off)
        forward[off] = remote(stepped.at[flat(cc, xx, zz)], everyone.at[me], f_send.at[i], f_recv.at[i],
                              device(zz, xx, cc, y))
    for off in offsets:
        if off[1] == 0:
            forward[off].start()
    everyone[me] = stepped[me]

    for copy in s_z:
        copy.wait()
    s_x = along_x(sampled, s_send, s_recv)
    s_x.start()
    for off in offsets:
        if off[1] != 0:
            forward[off].start()
    for copy in noise_z:
        copy.wait()
    n_x = along_x(noise, n_send, n_recv)
    n_x.start()
    s_x.wait()
    s_y = along_y(sampled, s_send, s_recv)
    s_y.start()
    n_x.wait()
    n_y = along_y(noise, n_send, n_recv)
    n_y.start()
    s_y.wait()
    s_c = along_core(sampled, s_send, s_recv)
    s_c.start()
    s_c.wait()

    dispersion = math.sqrt(widen_dispersion / (total - 1))
    for yy in range(ny):
        block = sampled[:, yy].reshape(total, obs)
        spread = dispersion * (block - jnp.sum(block, axis=0, keepdims=True) * (1.0 / total))
        hi, lo = halves(spread.T)
        st_hi[pl.ds(yy * obs, obs)] = hi
        st_lo[pl.ds(yy * obs, obs)] = lo

    nt = ((1,), (1,))
    every = ny * obs
    sth = st_hi[...]
    stl = st_lo[...]
    gram = dot3((sth, stl), (sth, stl), nt)
    ghi, glo = halves(gram)
    gram_hi[...] = ghi
    gram_lo[...] = glo
    upper = 1.0 + jnp.sqrt(jnp.sum(jnp.sum(gram * gram, axis=1, keepdims=True), axis=0, keepdims=True))
    theta = (upper + 1.0) / 2.0
    delta = (upper - 1.0) / 2.0
    sigma = theta / delta
    eye = jnp.where(
        lax.broadcasted_iota(jnp.int32, (every, every), 0) == lax.broadcasted_iota(jnp.int32, (every, every), 1),
        1.0, 0.0,
    )
    res[...] = eye
    start = eye * (1.0 / theta)
    direc[...] = start
    poly[...] = start

    n_y.wait()
    n_c = along_core(noise, n_send, n_recv)
    n_c.start()

    def turn(i, rho):
        d = direc[...]
        prod = dot3(halves(d), (gram_hi[...], gram_lo[...]))
        r = res[...] - d - prod
        res[...] = r
        rho_next = 1.0 / (2.0 * sigma - rho)
        d = (rho_next * rho) * d + (2.0 * rho_next / delta) * r
        direc[...] = d
        poly[...] = poly[...] + d
        return rho_next

    lax.fori_loop(0, CHEB - 1, turn, 1.0 / sigma)

    for off in offsets:
        forward[off].wait()
    n_c.wait()

    center = []
    devs = []
    for f in range(3):
        values = everyone[:, f].reshape(total, cols)
        mean = jnp.sum(values, axis=0, keepdims=True) * (1.0 / total)
        center.append(mean)
        devs.append(values - mean)
    dev = jnp.concatenate(devs, 1)
    cross = dot3((st_hi[...], st_lo[...]), halves(dev))
    weights = dispersion * dot3(halves(poly[...]), halves(cross))
    whi, wlo = halves(weights)

    def analyse(cc, xx, zz):
        at = flat(cc, xx, zz)
        innov = jnp.concatenate(
            [
                noise[cc, yy, xx, zz] - sampled[cc, yy, xx, zz]
                for yy in range(ny)
            ],
            1,
        )
        gain = dot3(halves(innov), (whi, wlo))
        for f in range(3):
            result[at, f] = (
                center[f]
                + math.sqrt(widen_dispersion) * (everyone[at, f] - center[f])
                + gain[:, f * cols : (f + 1) * cols]
            )
        return at

    back = []
    for i, off in enumerate(offsets):
        zz, xx, cc = shifted(off)
        at = analyse(cc, xx, zz)
        copy = remote(result.at[at], out_ref.at[me], b_send.at[i], b_recv.at[i], device(zz, xx, cc, y))
        copy.start()
        back.append(copy)
    at = analyse(c, x, z)
    out_ref[me] = result[at]
    for copy in back:
        copy.wait()


def with_halo(cells, sides, width):
    for axis, dim in sides:
        count = lax.axis_size(axis)
        head = lax.slice_in_dim(cells, 0, width, axis=dim)
        tail = lax.slice_in_dim(cells, cells.shape[dim] - width, cells.shape[dim], axis=dim)
        cells = jnp.concatenate(
            [
                lax.ppermute(tail, axis, [(i, (i + 1) % count) for i in range(count)]),
                cells,
                lax.ppermute(head, axis, [((i + 1) % count, i) for i in range(count)]),
            ],
            axis=dim,
        )
    return cells


def lax_friedrichs(state):
    depth = state[:, 0]
    east = state[:, 1]
    north = state[:, 2]
    press = 0.5 * gravity * depth * depth
    flux_x = jnp.stack([east, east * east / depth + press, east * north / depth], 1)
    flux_y = jnp.stack([north, east * north / depth, north * north / depth + press], 1)
    inner = state[:, :, 1:-1]
    average = 0.25 * (
        state[:, :, 2:] + state[:, :, :-2] + jnp.roll(inner, 1, 3) + jnp.roll(inner, -1, 3)
    )
    middle = flux_x[:, :, 1:-1]
    return (
        average
        - 0.5 * courant * (jnp.roll(middle, -1, 3) - jnp.roll(middle, 1, 3))
        - 0.5 * courant * (flux_y[:, :, 2:] - flux_y[:, :, :-2])
    )


def product(left, right):
    return jnp.dot(left, right, precision=lax.Precision.HIGHEST, preferred_element_type=jnp.float32)


def plain(
    prior_fields,
    measured_point_location,
    measured_depths,
    inverse_noise_deviation,
    sample_noise_draw,
    sample_line_labels,
):
    dispersion_multiplier = math.sqrt(widen_dispersion / (sample_noise_draw.shape[0] - 1))
    propagated_fields = prior_fields
    for step in range(STEPS):
        padded = with_halo(propagated_fields, (("run", 2),), 1)
        propagated_fields = lax_friedrichs(padded)
    members = propagated_fields.shape[0]
    depth_flat = propagated_fields[:, 0].reshape(
        members, propagated_fields.shape[2] * propagated_fields.shape[3]
    )
    sampled = inverse_noise_deviation[None, :] * jnp.take(
        depth_flat, measured_point_location, axis=1
    )
    innovation = (
        inverse_noise_deviation[None, :] * measured_depths[None, :]
        - sampled
        + jnp.take(sample_noise_draw, sample_line_labels, axis=0)
    )
    all_sampled, all_innov = (
        lax.all_gather(sampled, ("role", "grp"), axis=0, tiled=True),
        lax.all_gather(innovation, ("role", "grp"), axis=0, tiled=True),
    )
    spread = dispersion_multiplier * (all_sampled - jnp.mean(all_sampled, axis=0, keepdims=True))
    first = lax.axis_index(("role", "grp")) * members
    own_spread = lax.dynamic_slice_in_dim(spread, first, members, 0)
    own_innov = lax.dynamic_slice_in_dim(all_innov, first, members, 0)
    gram_rows, cross_rows = (
        lax.psum_scatter(product(own_spread, spread.T), "run", scatter_dimension=0, tiled=True),
        lax.psum_scatter(product(own_innov, spread.T), "run", scatter_dimension=0, tiled=True),
    )
    gram = lax.all_gather(gram_rows, ("role", "grp", "run"), axis=0, tiled=True)
    upper = 1.0 + jnp.sqrt(jnp.sum(gram * gram))
    theta = (upper + 1.0) / 2.0
    delta = (upper - 1.0) / 2.0
    sigma = theta / delta
    rho = 1.0 / sigma
    residual = cross_rows
    direction = residual / theta
    linear_solution = direction
    for turn in range(CHEB - 1):
        residual = residual - direction - product(direction, gram)
        rho_next = 1.0 / (2.0 * sigma - rho)
        direction = rho_next * rho * direction + 2.0 * rho_next / delta * residual
        linear_solution = linear_solution + direction
        rho = rho_next
    posterior_coefficients = lax.all_gather(
        linear_solution, ("role", "grp", "run"), axis=0, tiled=True
    )
    ensemble_combination = (
        math.sqrt(widen_dispersion) * jnp.eye(posterior_coefficients.shape[0], dtype=jnp.float32)
        + dispersion_multiplier * posterior_coefficients
    )
    strip_slab = lax.all_to_all(
        propagated_fields, ("role", "grp"), split_axis=2, concat_axis=0, tiled=True
    )
    array_shape = strip_slab.shape
    flat = strip_slab.reshape(array_shape[0], array_shape[1] * array_shape[2] * array_shape[3])
    center = jnp.mean(flat, axis=0, keepdims=True)
    updated = (center + product(ensemble_combination, flat - center)).reshape(array_shape)
    return lax.all_to_all(updated, ("role", "grp"), split_axis=0, concat_axis=2, tiled=True)


def fused(
    dims,
    prior_fields,
    measured_point_location,
    measured_depths,
    inverse_noise_deviation,
    sample_noise_draw,
    sample_line_labels,
):
    nz, nx, nc, ny = dims
    members, _, rows, cols = prior_fields.shape
    obs = measured_point_location.shape[0]
    every = ny * obs
    group = nz * nx * nc
    slab = (group, 3, members, cols)
    target = inverse_noise_deviation[None, :] * measured_depths[None, :] + jnp.take(
        sample_noise_draw, sample_line_labels, axis=0
    )
    gathered = (nc, ny, nx, nz, members, obs)
    dma = pltpu.SemaphoreType.DMA
    out = pl.pallas_call(
        functools.partial(kernel, dims),
        out_shape=jax.ShapeDtypeStruct(slab, jnp.float32),
        in_specs=[pl.BlockSpec(memory_space=pltpu.VMEM)] * 4,
        out_specs=pl.BlockSpec(memory_space=pltpu.VMEM),
        scratch_shapes=[
            pltpu.VMEM((2, STEPS, 3, members, cols), jnp.float32),
            pltpu.VMEM(slab, jnp.float32),
            pltpu.VMEM(slab, jnp.float32),
            pltpu.VMEM(slab, jnp.float32),
            pltpu.VMEM(gathered, jnp.float32),
            pltpu.VMEM(gathered, jnp.float32),
            pltpu.VMEM((every, group * members), jnp.bfloat16),
            pltpu.VMEM((every, group * members), jnp.bfloat16),
            pltpu.VMEM((every, every), jnp.bfloat16),
            pltpu.VMEM((every, every), jnp.bfloat16),
            pltpu.VMEM((every, every), jnp.float32),
            pltpu.VMEM((every, every), jnp.float32),
            pltpu.VMEM((every, every), jnp.float32),
            dma((2 * CHUNKS,)),
            dma((2 * CHUNKS,)),
            dma((nz + 3,)),
            dma((nz + 3,)),
            dma((nz + 3,)),
            dma((nz + 3,)),
            dma((group,)),
            dma((group,)),
            dma((group,)),
            dma((group,)),
        ],
        compiler_params=pltpu.CompilerParams(
            collective_id=0, has_side_effects=True, vmem_limit_bytes=60 * 1024 * 1024
        ),
        name="analysis_kernel",
    )(
        prior_fields.transpose(2, 1, 0, 3),
        measured_point_location[None, :],
        inverse_noise_deviation[None, :],
        target,
    )
    return out.transpose(2, 1, 0, 3)


def shards(shape, *args):
    nz, grp, ny = shape["role"], shape["grp"], shape["run"]
    members, _, rows, cols = args[0].shape
    fits = (
        grp == 4
        and ny == 2
        and rows == nz * grp
        and members % (CHUNKS * TILE) == 0
        and cols == 128
        and args[1].shape[0] * ny <= 512
    )
    if fits:
        return fused((nz, 2, 2, ny), *args)
    return plain(*args)


def solution(mesh):
    placed = (
        P(("role", "grp"), None, "run", None),
        P("run"),
        P("run"),
        P("run"),
        P(None, "run"),
        P(("role", "grp")),
    )
    return jax.shard_map(
        functools.partial(shards, dict(mesh.shape)),
        mesh=mesh,
        in_specs=placed,
        out_specs=P(("role", "grp"), None, "run", None),
        check_vma=False,
    )
```

```python
import functools
import math

import jax
import jax.numpy as jnp
from jax import lax
from jax.experimental import pallas as pl
from jax.experimental.pallas import tpu as pltpu
from jax.sharding import PartitionSpec as P

STEPS = 4
CHEB = 8
CHUNKS = 4
TILE = 8

gravity = 1.0
courant = 0.35
widen_dispersion = 1.1

MESH = pl.DeviceIdType.MESH


def advance(fields):
    depth, east, north = fields
    half = 0.5 * courant
    inverse = 1.0 / depth
    press = 0.5 * gravity * depth * depth
    speed_x = east * inverse
    speed_y = north * inverse
    mixed = east * speed_y
    flux_x = (east, east * speed_x + press, mixed)
    flux_y = (north, mixed, north * speed_y + press)
    rows = depth.shape[0]
    out = []
    for q, fx, fy in zip(fields, flux_x, flux_y):
        quarter = 0.25 * q
        mid = quarter[1:-1]
        kx = half * fx[1:-1]
        sides = pltpu.roll(mid - kx, q.shape[2] - 1, 2) + pltpu.roll(mid + kx, 1, 2)
        up = (quarter - half * fy)[2:]
        down = (quarter + half * fy)[: rows - 2]
        out.append(sides + up + down)
    return tuple(out)


def halves(value):
    high = value.astype(jnp.bfloat16)
    return high, (value - high.astype(jnp.float32)).astype(jnp.bfloat16)


def dot(left, right, dims=((1,), (0,))):
    return lax.dot_general(left, right, (dims, ((), ())), preferred_element_type=jnp.float32)


def dot3(left, right, dims=((1,), (0,))):
    (lh, ll), (rh, rl) = left, right
    return dot(lh, rh, dims) + (dot(lh, rl, dims) + dot(ll, rh, dims))


def kernel(
    dims,
    label_ref, x_ref, loc_ref, inv_ref, meas_ref, table_ref,
    out_ref,
    halo, stepped, everyone, result, sampled, noise, hot,
    st_hi, st_lo, gram_hi, gram_lo, res, direc, poly,
    halo_send, halo_recv, s_send, s_recv, n_send, n_recv, f_send, f_recv, b_send, b_recv,
):
    nz, nx, nc, ny = dims
    z = lax.axis_index("role")
    grp = lax.axis_index("grp")
    y = lax.axis_index("run")
    x = grp // nc
    c = grp % nc
    rows, _, members, cols = x_ref.shape
    obs = loc_ref.shape[1]
    total = nz * nx * nc * members
    width = halo.shape[1]

    def device(zz, xx, cc, yy):
        return (zz, xx * nc + cc, yy)

    def flat(cc, xx, zz):
        return (cc * nx + xx) * nz + zz

    me = flat(c, x, z)
    offsets = [(dz, dx, dc) for dz in range(nz) for dx in range(nx) for dc in range(nc)][1:]
    far = {0: 0, nz // 2: 2}
    offsets.sort(key=lambda o: (-far.get(o[0], 1), o[0], -o[1], -o[2]))

    def shifted(off):
        dz, dx, dc = off
        return lax.rem(z + dz, nz), lax.rem(x + dx, nx), lax.rem(c + dc, nc)

    other_y = lax.rem(y + 1, ny)

    barrier = pltpu.get_barrier_semaphore()
    for off in offsets:
        zz, xx, cc = shifted(off)
        pl.semaphore_signal(barrier, inc=1, device_id=device(zz, xx, cc, y), device_id_type=MESH)
    pl.semaphore_signal(barrier, inc=1, device_id=device(z, x, c, other_y), device_id_type=MESH)
    pl.semaphore_wait(barrier, len(offsets) + 1)

    def remote(src, dst, send, recv, target):
        return pltpu.make_async_remote_copy(
            src_ref=src, dst_ref=dst, send_sem=send, recv_sem=recv, device_id=target, device_id_type=MESH
        )

    per = members // CHUNKS
    halo_copies = []
    for k in range(CHUNKS):
        part = pl.ds(k * per, per)
        pair = (
            remote(x_ref.at[pl.ds(rows - width, width), :, part], halo.at[0, :, :, part],
                   halo_send.at[2 * k], halo_recv.at[2 * k], device(z, x, c, other_y)),
            remote(x_ref.at[pl.ds(0, width), :, part], halo.at[1, :, :, part],
                   halo_send.at[2 * k + 1], halo_recv.at[2 * k + 1], device(z, x, c, other_y)),
        )
        for copy in pair:
            copy.start()
        halo_copies.append(pair)

    xo = lax.rem(x + 1, nx)
    co = lax.rem(c + 1, nc)
    east_side = device(z, xo, c, y)
    north_side = device(z, x, c, other_y)
    twin = device(z, x, co, y)
    hops = nz - 1

    class Gather:
        def __init__(self, buf, send, recv, base, part):
            self.buf, self.send, self.recv, self.base, self.part = buf, send, recv, base, part
            self.open = {}

        def go(self, name, slot, line, one, target):
            yy, xx = line
            where = (c, yy, xx, z, self.part) if one else (c, yy, xx, slice(None), self.part)
            piece = self.buf.at[where]
            copy = remote(piece, piece, self.send.at[self.base + slot], self.recv.at[self.base + slot], target)
            copy.start()
            self.open[name] = copy

        def take(self, name):
            self.open.pop(name).wait()

        def first(self):
            for d in range(1, nz):
                self.go(("z", d), d - 1, (y, x), True, device(lax.rem(z + d, nz), x, c, y))

        def spread(self, north=True):
            for d in range(1, nz):
                self.take(("z", d))
            if north:
                self.north()
            self.go("x", hops + 1, (y, x), False, east_side)
            self.go("c0", hops + 3, (y, x), False, twin)

        def north(self):
            self.go("y", hops, (y, x), False, north_side)

        def relay_east(self):
            self.take("x")
            self.go("c1", hops + 4, (y, xo), False, twin)

        def relay_north(self):
            self.take("y")
            self.go("xo", hops + 2, (other_y, x), False, east_side)
            self.go("c2", hops + 5, (other_y, x), False, twin)

        def relay_last(self):
            self.take("xo")
            self.go("c3", hops + 6, (other_y, xo), False, twin)

        def finish(self):
            for name in list(self.open):
                self.take(name)

    def fetch(i, carry):
        noise[c, y, x, z, pl.ds(i, 1)] = table_ref[pl.ds(label_ref[i], 1)]
        return carry

    lax.fori_loop(0, members, fetch, 0)
    noise[c, y, x, z] = noise[c, y, x, z] + inv_ref[...] * meas_ref[...]
    noise_gather = Gather(noise, n_send, n_recv, 0, slice(None))
    noise_gather.first()

    loc = loc_ref[...]
    lanes = lax.broadcasted_iota(jnp.int32, (cols, obs), 0)

    def mark(r, carry):
        at = pl.ds(pl.multiple_of(r * cols, cols), cols)
        hot[at] = jnp.where(loc - r * cols == lanes, 1.0, 0.0).astype(jnp.bfloat16)
        return carry

    lax.fori_loop(0, rows, mark, 0)
    noise_gather.spread(north=False)

    gathers = []
    forward = []
    for k in range(CHUNKS):
        for copy in halo_copies[k]:
            copy.wait()

        def tile(t, carry):
            at = pl.ds(pl.multiple_of(k * per + t * TILE, TILE), TILE)
            fields = tuple(
                jnp.concatenate([halo[0, :, f, at], x_ref[:, f, at], halo[1, :, f, at]], 0) for f in range(3)
            )
            for step in range(STEPS):
                fields = advance(fields)
            for f in range(3):
                stepped[:, f, at] = fields[f]
            return carry

        lax.fori_loop(0, per // TILE, tile, 0)

        part = pl.ds(k * per, per)
        depth = jnp.concatenate([stepped[r, 0, part] for r in range(rows)], 1)
        d1 = depth.astype(jnp.bfloat16)
        rest = depth - d1.astype(jnp.float32)
        d2 = rest.astype(jnp.bfloat16)
        d3 = (rest - d2.astype(jnp.float32)).astype(jnp.bfloat16)
        found = dot(jnp.concatenate([d1, d2, d3], 0), hot[...])
        found = found[:per] + (found[per : 2 * per] + found[2 * per :])
        sampled[c, y, x, z, part] = inv_ref[...] * found
        gather = Gather(sampled, s_send, s_recv, k * (hops + 7), part)
        gather.first()
        gathers.append(gather)
        if k > 0:
            gathers[k - 1].spread()
        for i, off in enumerate(offsets):
            zz, xx, cc = shifted(off)
            copy = remote(stepped.at[flat(cc, xx, zz), :, part], everyone.at[me, :, part],
                          f_send.at[k * len(offsets) + i], f_recv.at[k * len(offsets) + i], device(zz, xx, cc, y))
            copy.start()
            forward.append(copy)

    gathers[-1].spread()
    everyone[me] = stepped[me]
    for gather in gathers:
        gather.relay_north()
    for gather in gathers:
        gather.relay_east()
    noise_gather.north()
    noise_gather.relay_east()
    for gather in gathers:
        gather.relay_last()
    for gather in gathers:
        gather.finish()

    dispersion = math.sqrt(widen_dispersion / (total - 1))
    for yy in range(ny):
        block = sampled[:, yy].reshape(total, obs)
        spread = dispersion * (block - jnp.sum(block, axis=0, keepdims=True) * (1.0 / total))
        hi, lo = halves(spread.T)
        st_hi[pl.ds(yy * obs, obs)] = hi
        st_lo[pl.ds(yy * obs, obs)] = lo

    nt = ((1,), (1,))
    every = ny * obs
    sth = st_hi[...]
    stl = st_lo[...]
    gram = dot3((sth, stl), (sth, stl), nt)
    ghi, glo = halves(gram)
    gram_hi[...] = ghi
    gram_lo[...] = glo
    upper = 1.0 + jnp.sqrt(jnp.sum(jnp.sum(gram * gram, axis=1, keepdims=True), axis=0, keepdims=True))
    theta = (upper + 1.0) / 2.0
    delta = (upper - 1.0) / 2.0
    sigma = theta / delta
    eye = jnp.where(
        lax.broadcasted_iota(jnp.int32, (every, every), 0) == lax.broadcasted_iota(jnp.int32, (every, every), 1),
        1.0, 0.0,
    )
    res[...] = eye
    start = eye * (1.0 / theta)
    direc[...] = start
    poly[...] = start

    noise_gather.relay_north()

    def turn(i, rho):
        d = direc[...]
        prod = dot3(halves(d), (gram_hi[...], gram_lo[...]))
        r = res[...] - d - prod
        res[...] = r
        rho_next = 1.0 / (2.0 * sigma - rho)
        d = (rho_next * rho) * d + (2.0 * rho_next / delta) * r
        direc[...] = d
        poly[...] = poly[...] + d
        return rho_next

    lax.fori_loop(0, CHEB - 1, turn, 1.0 / sigma)

    noise_gather.relay_last()
    for copy in forward:
        copy.wait()
    noise_gather.finish()

    center = []
    devs = []
    for f in range(3):
        values = everyone[:, f].reshape(total, cols)
        mean = jnp.sum(values, axis=0, keepdims=True) * (1.0 / total)
        center.append(mean)
        devs.append(values - mean)
    dev = jnp.concatenate(devs, 1)
    cross = dot3((st_hi[...], st_lo[...]), halves(dev))
    weights = dispersion * dot3(halves(poly[...]), halves(cross))
    whi, wlo = halves(weights)

    def analyse(places):
        innov = jnp.concatenate(
            [
                jnp.concatenate([noise[cc, yy, xx, zz] - sampled[cc, yy, xx, zz] for yy in range(ny)], 1)
                for zz, xx, cc in places
            ],
            0,
        )
        high, low = halves(innov)
        count = innov.shape[0]
        both = dot(jnp.concatenate([high, low], 0), whi)
        gain = both[:count] + (both[count:] + dot(high, wlo))
        for n, (zz, xx, cc) in enumerate(places):
            at = flat(cc, xx, zz)
            for f in range(3):
                result[at, f] = (
                    center[f]
                    + math.sqrt(widen_dispersion) * (everyone[at, f] - center[f])
                    + gain[n * members : (n + 1) * members, f * cols : (f + 1) * cols]
                )

    back = []
    order = offsets + [(0, 0, 0)]
    batch = nx * nc
    for b in range(0, len(order), batch):
        some = order[b : b + batch]
        analyse([shifted(off) for off in some])
        for n, off in enumerate(some):
            if off == (0, 0, 0):
                continue
            zz, xx, cc = shifted(off)
            copy = remote(result.at[flat(cc, xx, zz)], out_ref.at[me], b_send.at[b + n], b_recv.at[b + n],
                          device(zz, xx, cc, y))
            copy.start()
            back.append(copy)
    out_ref[me] = result[me]
    for copy in back:
        copy.wait()


def with_halo(cells, sides, width):
    for axis, dim in sides:
        count = lax.axis_size(axis)
        head = lax.slice_in_dim(cells, 0, width, axis=dim)
        tail = lax.slice_in_dim(cells, cells.shape[dim] - width, cells.shape[dim], axis=dim)
        cells = jnp.concatenate(
            [
                lax.ppermute(tail, axis, [(i, (i + 1) % count) for i in range(count)]),
                cells,
                lax.ppermute(head, axis, [((i + 1) % count, i) for i in range(count)]),
            ],
            axis=dim,
        )
    return cells


def lax_friedrichs(state):
    depth = state[:, 0]
    east = state[:, 1]
    north = state[:, 2]
    press = 0.5 * gravity * depth * depth
    flux_x = jnp.stack([east, east * east / depth + press, east * north / depth], 1)
    flux_y = jnp.stack([north, east * north / depth, north * north / depth + press], 1)
    inner = state[:, :, 1:-1]
    average = 0.25 * (
        state[:, :, 2:] + state[:, :, :-2] + jnp.roll(inner, 1, 3) + jnp.roll(inner, -1, 3)
    )
    middle = flux_x[:, :, 1:-1]
    return (
        average
        - 0.5 * courant * (jnp.roll(middle, -1, 3) - jnp.roll(middle, 1, 3))
        - 0.5 * courant * (flux_y[:, :, 2:] - flux_y[:, :, :-2])
    )


def product(left, right):
    return jnp.dot(left, right, precision=lax.Precision.HIGHEST, preferred_element_type=jnp.float32)


def plain(
    prior_fields,
    measured_point_location,
    measured_depths,
    inverse_noise_deviation,
    sample_noise_draw,
    sample_line_labels,
):
    dispersion_multiplier = math.sqrt(widen_dispersion / (sample_noise_draw.shape[0] - 1))
    propagated_fields = prior_fields
    for step in range(STEPS):
        padded = with_halo(propagated_fields, (("run", 2),), 1)
        propagated_fields = lax_friedrichs(padded)
    members = propagated_fields.shape[0]
    depth_flat = propagated_fields[:, 0].reshape(
        members, propagated_fields.shape[2] * propagated_fields.shape[3]
    )
    sampled = inverse_noise_deviation[None, :] * jnp.take(
        depth_flat, measured_point_location, axis=1
    )
    innovation = (
        inverse_noise_deviation[None, :] * measured_depths[None, :]
        - sampled
        + jnp.take(sample_noise_draw, sample_line_labels, axis=0)
    )
    all_sampled, all_innov = (
        lax.all_gather(sampled, ("role", "grp"), axis=0, tiled=True),
        lax.all_gather(innovation, ("role", "grp"), axis=0, tiled=True),
    )
    spread = dispersion_multiplier * (all_sampled - jnp.mean(all_sampled, axis=0, keepdims=True))
    first = lax.axis_index(("role", "grp")) * members
    own_spread = lax.dynamic_slice_in_dim(spread, first, members, 0)
    own_innov = lax.dynamic_slice_in_dim(all_innov, first, members, 0)
    gram_rows, cross_rows = (
        lax.psum_scatter(product(own_spread, spread.T), "run", scatter_dimension=0, tiled=True),
        lax.psum_scatter(product(own_innov, spread.T), "run", scatter_dimension=0, tiled=True),
    )
    gram = lax.all_gather(gram_rows, ("role", "grp", "run"), axis=0, tiled=True)
    upper = 1.0 + jnp.sqrt(jnp.sum(gram * gram))
    theta = (upper + 1.0) / 2.0
    delta = (upper - 1.0) / 2.0
    sigma = theta / delta
    rho = 1.0 / sigma
    residual = cross_rows
    direction = residual / theta
    linear_solution = direction
    for turn in range(CHEB - 1):
        residual = residual - direction - product(direction, gram)
        rho_next = 1.0 / (2.0 * sigma - rho)
        direction = rho_next * rho * direction + 2.0 * rho_next / delta * residual
        linear_solution = linear_solution + direction
        rho = rho_next
    posterior_coefficients = lax.all_gather(
        linear_solution, ("role", "grp", "run"), axis=0, tiled=True
    )
    ensemble_combination = (
        math.sqrt(widen_dispersion) * jnp.eye(posterior_coefficients.shape[0], dtype=jnp.float32)
        + dispersion_multiplier * posterior_coefficients
    )
    strip_slab = lax.all_to_all(
        propagated_fields, ("role", "grp"), split_axis=2, concat_axis=0, tiled=True
    )
    array_shape = strip_slab.shape
    flat = strip_slab.reshape(array_shape[0], array_shape[1] * array_shape[2] * array_shape[3])
    center = jnp.mean(flat, axis=0, keepdims=True)
    updated = (center + product(ensemble_combination, flat - center)).reshape(array_shape)
    return lax.all_to_all(updated, ("role", "grp"), split_axis=0, concat_axis=2, tiled=True)


def fused(
    dims,
    prior_fields,
    measured_point_location,
    measured_depths,
    inverse_noise_deviation,
    sample_noise_draw,
    sample_line_labels,
):
    nz, nx, nc, ny = dims
    members, _, rows, cols = prior_fields.shape
    obs = measured_point_location.shape[0]
    every = ny * obs
    group = nz * nx * nc
    slab = (group, 3, members, cols)
    gathered = (nc, ny, nx, nz, members, obs)
    dma = pltpu.SemaphoreType.DMA
    out = pl.pallas_call(
        functools.partial(kernel, dims),
        out_shape=jax.ShapeDtypeStruct(slab, jnp.float32),
        in_specs=[pl.BlockSpec(memory_space=pltpu.SMEM)] + [pl.BlockSpec(memory_space=pltpu.VMEM)] * 5,
        out_specs=pl.BlockSpec(memory_space=pltpu.VMEM),
        scratch_shapes=[
            pltpu.VMEM((2, STEPS, 3, members, cols), jnp.float32),
            pltpu.VMEM(slab, jnp.float32),
            pltpu.VMEM(slab, jnp.float32),
            pltpu.VMEM(slab, jnp.float32),
            pltpu.VMEM(gathered, jnp.float32),
            pltpu.VMEM(gathered, jnp.float32),
            pltpu.VMEM((rows * cols, obs), jnp.bfloat16),
            pltpu.VMEM((every, group * members), jnp.bfloat16),
            pltpu.VMEM((every, group * members), jnp.bfloat16),
            pltpu.VMEM((every, every), jnp.bfloat16),
            pltpu.VMEM((every, every), jnp.bfloat16),
            pltpu.VMEM((every, every), jnp.float32),
            pltpu.VMEM((every, every), jnp.float32),
            pltpu.VMEM((every, every), jnp.float32),
            dma((2 * CHUNKS,)),
            dma((2 * CHUNKS,)),
            dma((CHUNKS * (nz + 6),)),
            dma((CHUNKS * (nz + 6),)),
            dma((nz + 6,)),
            dma((nz + 6,)),
            dma((CHUNKS * group,)),
            dma((CHUNKS * group,)),
            dma((group,)),
            dma((group,)),
        ],
        compiler_params=pltpu.CompilerParams(
            collective_id=0, has_side_effects=True, vmem_limit_bytes=60 * 1024 * 1024
        ),
        name="analysis_kernel",
    )(
        sample_line_labels,
        prior_fields.transpose(2, 1, 0, 3),
        measured_point_location[None, :],
        inverse_noise_deviation[None, :],
        measured_depths[None, :],
        sample_noise_draw,
    )
    return out.transpose(2, 1, 0, 3)


def shards(shape, *args):
    nz, grp, ny = shape["role"], shape["grp"], shape["run"]
    members, _, rows, cols = args[0].shape
    fits = (
        grp == 4
        and ny == 2
        and rows == nz * grp
        and members % (CHUNKS * TILE) == 0
        and cols == 128
        and args[1].shape[0] * ny <= 512
    )
    if fits:
        return fused((nz, 2, 2, ny), *args)
    return plain(*args)


def solution(mesh):
    placed = (
        P(("role", "grp"), None, "run", None),
        P("run"),
        P("run"),
        P("run"),
        P(None, "run"),
        P(("role", "grp")),
    )
    return jax.shard_map(
        functools.partial(shards, dict(mesh.shape)),
        mesh=mesh,
        in_specs=placed,
        out_specs=P(("role", "grp"), None, "run", None),
        check_vma=False,
    )
```

```python
import functools
import math

import jax
import jax.numpy as jnp
from jax import lax
from jax.experimental import pallas as pl
from jax.experimental.pallas import tpu as pltpu
from jax.sharding import PartitionSpec as P

STEPS = 4
CHEB = 8
CHUNKS = 4
TILE = 8

gravity = 1.0
courant = 0.35
widen_dispersion = 1.1

MESH = pl.DeviceIdType.MESH


def advance(fields):
    depth, east, north = fields
    half = 0.5 * courant
    inverse = 1.0 / depth
    press = 0.5 * gravity * depth * depth
    speed_x = east * inverse
    speed_y = north * inverse
    mixed = east * speed_y
    flux_x = (east, east * speed_x + press, mixed)
    flux_y = (north, mixed, north * speed_y + press)
    rows = depth.shape[0]
    out = []
    for q, fx, fy in zip(fields, flux_x, flux_y):
        quarter = 0.25 * q
        mid = quarter[1:-1]
        kx = half * fx[1:-1]
        sides = pltpu.roll(mid - kx, q.shape[2] - 1, 2) + pltpu.roll(mid + kx, 1, 2)
        up = (quarter - half * fy)[2:]
        down = (quarter + half * fy)[: rows - 2]
        out.append(sides + up + down)
    return tuple(out)


def halves(value):
    high = value.astype(jnp.bfloat16)
    return high, (value - high.astype(jnp.float32)).astype(jnp.bfloat16)


def dot(left, right, dims=((1,), (0,))):
    return lax.dot_general(left, right, (dims, ((), ())), preferred_element_type=jnp.float32)


def dot3(left, right, dims=((1,), (0,))):
    (lh, ll), (rh, rl) = left, right
    return dot(lh, rh, dims) + (dot(lh, rl, dims) + dot(ll, rh, dims))


def kernel(
    dims,
    label_ref, x_ref, loc_ref, inv_ref, meas_ref, table_ref,
    out_ref,
    halo, stepped, everyone, result, sampled, noise, hot,
    st_hi, st_lo, gram_hi, gram_lo, res, direc, poly,
    halo_send, halo_recv, s_send, s_recv, n_send, n_recv, f_send, f_recv, b_send, b_recv,
):
    nz, nx, nc, ny = dims
    z = lax.axis_index("role")
    grp = lax.axis_index("grp")
    y = lax.axis_index("run")
    x = grp // nc
    c = grp % nc
    rows, _, members, cols = x_ref.shape
    obs = loc_ref.shape[1]
    total = nz * nx * nc * members
    width = halo.shape[1]

    def device(zz, xx, cc, yy):
        return (zz, xx * nc + cc, yy)

    def flat(cc, xx, zz):
        return (cc * nx + xx) * nz + zz

    me = flat(c, x, z)
    offsets = [(dz, dx, dc) for dz in range(nz) for dx in range(nx) for dc in range(nc)][1:]
    far = {0: 0, nz // 2: 2}
    offsets.sort(key=lambda o: (-far.get(o[0], 1), o[0], -o[1], -o[2]))

    def shifted(off):
        dz, dx, dc = off
        return lax.rem(z + dz, nz), lax.rem(x + dx, nx), lax.rem(c + dc, nc)

    other_y = lax.rem(y + 1, ny)

    barrier = pltpu.get_barrier_semaphore()
    for off in offsets:
        zz, xx, cc = shifted(off)
        pl.semaphore_signal(barrier, inc=1, device_id=device(zz, xx, cc, y), device_id_type=MESH)
    pl.semaphore_signal(barrier, inc=1, device_id=device(z, x, c, other_y), device_id_type=MESH)
    pl.semaphore_wait(barrier, len(offsets) + 1)

    def remote(src, dst, send, recv, target):
        return pltpu.make_async_remote_copy(
            src_ref=src, dst_ref=dst, send_sem=send, recv_sem=recv, device_id=target, device_id_type=MESH
        )

    per = members // CHUNKS
    halo_copies = []
    for k in range(CHUNKS):
        part = pl.ds(k * per, per)
        pair = (
            remote(x_ref.at[pl.ds(rows - width, width), :, part], halo.at[0, :, :, part],
                   halo_send.at[2 * k], halo_recv.at[2 * k], device(z, x, c, other_y)),
            remote(x_ref.at[pl.ds(0, width), :, part], halo.at[1, :, :, part],
                   halo_send.at[2 * k + 1], halo_recv.at[2 * k + 1], device(z, x, c, other_y)),
        )
        for copy in pair:
            copy.start()
        halo_copies.append(pair)

    xo = lax.rem(x + 1, nx)
    co = lax.rem(c + 1, nc)
    east_side = device(z, xo, c, y)
    north_side = device(z, x, c, other_y)
    twin = device(z, x, co, y)
    hops = nz - 1

    class Gather:
        def __init__(self, buf, send, recv, base, part):
            self.buf, self.send, self.recv, self.base, self.part = buf, send, recv, base, part
            self.open = {}

        def go(self, name, slot, line, one, target):
            yy, xx = line
            where = (c, yy, xx, z, self.part) if one else (c, yy, xx, slice(None), self.part)
            piece = self.buf.at[where]
            copy = remote(piece, piece, self.send.at[self.base + slot], self.recv.at[self.base + slot], target)
            copy.start()
            self.open[name] = copy

        def take(self, name):
            self.open.pop(name).wait()

        def first(self):
            for d in range(1, nz):
                self.go(("z", d), d - 1, (y, x), True, device(lax.rem(z + d, nz), x, c, y))

        def spread(self, north=True):
            for d in range(1, nz):
                self.take(("z", d))
            if north:
                self.north()
            self.go("x", hops + 1, (y, x), False, east_side)
            self.go("c0", hops + 3, (y, x), False, twin)

        def north(self):
            self.go("y", hops, (y, x), False, north_side)

        def relay_east(self):
            self.take("x")
            self.go("c1", hops + 4, (y, xo), False, twin)

        def relay_north(self):
            self.take("y")
            self.go("xo", hops + 2, (other_y, x), False, east_side)
            self.go("c2", hops + 5, (other_y, x), False, twin)

        def relay_last(self):
            self.take("xo")
            self.go("c3", hops + 6, (other_y, xo), False, twin)

        def finish(self):
            for name in list(self.open):
                self.take(name)

    def fetch(i, carry):
        noise[c, y, x, z, pl.ds(i, 1)] = table_ref[pl.ds(label_ref[i], 1)]
        return carry

    lax.fori_loop(0, members, fetch, 0)
    noise[c, y, x, z] = noise[c, y, x, z] + inv_ref[...] * meas_ref[...]
    noise_gather = Gather(noise, n_send, n_recv, 0, slice(None))
    noise_gather.first()

    loc = loc_ref[...]
    lanes = lax.broadcasted_iota(jnp.int32, (cols, obs), 0)

    def mark(r, carry):
        at = pl.ds(pl.multiple_of(r * cols, cols), cols)
        hot[at] = jnp.where(loc - r * cols == lanes, 1.0, 0.0).astype(jnp.bfloat16)
        return carry

    lax.fori_loop(0, rows, mark, 0)
    noise_gather.spread(north=False)

    gathers = []
    forward = []
    early = (0, nz // 2)

    def ship(off, part, slot):
        zz, xx, cc = shifted(off)
        copy = remote(stepped.at[flat(cc, xx, zz), :, part], everyone.at[me, :, part],
                      f_send.at[slot], f_recv.at[slot], device(zz, xx, cc, y))
        copy.start()
        forward.append(copy)

    def ship_early(k, part):
        for i, off in enumerate(offsets):
            if off[0] in early:
                ship(off, part, k * len(offsets) + i)

    def ship_late(dx):
        for i, off in enumerate(offsets):
            if off[0] not in early and off[1] == dx:
                ship(off, slice(None), i)
    for k in range(CHUNKS):
        for copy in halo_copies[k]:
            copy.wait()

        def tile(t, carry):
            at = pl.ds(pl.multiple_of(k * per + t * TILE, TILE), TILE)
            fields = tuple(
                jnp.concatenate([halo[0, :, f, at], x_ref[:, f, at], halo[1, :, f, at]], 0) for f in range(3)
            )
            for step in range(STEPS):
                fields = advance(fields)
            for f in range(3):
                stepped[:, f, at] = fields[f]
            return carry

        lax.fori_loop(0, per // TILE, tile, 0)

        part = pl.ds(k * per, per)
        depth = jnp.concatenate([stepped[r, 0, part] for r in range(rows)], 1)
        d1 = depth.astype(jnp.bfloat16)
        rest = depth - d1.astype(jnp.float32)
        d2 = rest.astype(jnp.bfloat16)
        d3 = (rest - d2.astype(jnp.float32)).astype(jnp.bfloat16)
        found = dot(jnp.concatenate([d1, d2, d3], 0), hot[...])
        found = found[:per] + (found[per : 2 * per] + found[2 * per :])
        sampled[c, y, x, z, part] = inv_ref[...] * found
        gather = Gather(sampled, s_send, s_recv, k * (hops + 7), part)
        gather.first()
        gathers.append(gather)
        if k > 0:
            gathers[k - 1].spread()
        if k < CHUNKS - 1:
            ship_early(k, part)

    gathers[-1].spread()
    ship_early(CHUNKS - 1, pl.ds((CHUNKS - 1) * per, per))
    ship_late(0)
    everyone[me] = stepped[me]
    for gather in gathers:
        gather.relay_north()
    ship_late(1)
    for gather in gathers:
        gather.relay_east()
    noise_gather.north()
    noise_gather.relay_east()
    for gather in gathers:
        gather.relay_last()
    for gather in gathers:
        gather.finish()

    dispersion = math.sqrt(widen_dispersion / (total - 1))
    for yy in range(ny):
        block = sampled[:, yy].reshape(total, obs)
        spread = dispersion * (block - jnp.sum(block, axis=0, keepdims=True) * (1.0 / total))
        hi, lo = halves(spread.T)
        st_hi[pl.ds(yy * obs, obs)] = hi
        st_lo[pl.ds(yy * obs, obs)] = lo

    nt = ((1,), (1,))
    every = ny * obs
    sth = st_hi[...]
    stl = st_lo[...]
    gram = dot3((sth, stl), (sth, stl), nt)
    ghi, glo = halves(gram)
    gram_hi[...] = ghi
    gram_lo[...] = glo
    upper = 1.0 + jnp.sqrt(jnp.sum(jnp.sum(gram * gram, axis=1, keepdims=True), axis=0, keepdims=True))
    theta = (upper + 1.0) / 2.0
    delta = (upper - 1.0) / 2.0
    sigma = theta / delta
    eye = jnp.where(
        lax.broadcasted_iota(jnp.int32, (every, every), 0) == lax.broadcasted_iota(jnp.int32, (every, every), 1),
        1.0, 0.0,
    )
    res[...] = eye
    start = eye * (1.0 / theta)
    direc[...] = start
    poly[...] = start

    noise_gather.relay_north()

    def turn(i, rho):
        d = direc[...]
        prod = dot3(halves(d), (gram_hi[...], gram_lo[...]))
        r = res[...] - d - prod
        res[...] = r
        rho_next = 1.0 / (2.0 * sigma - rho)
        d = (rho_next * rho) * d + (2.0 * rho_next / delta) * r
        direc[...] = d
        poly[...] = poly[...] + d
        return rho_next

    lax.fori_loop(0, CHEB - 1, turn, 1.0 / sigma)

    noise_gather.relay_last()
    for copy in forward:
        copy.wait()
    noise_gather.finish()

    center = []
    devs = []
    for f in range(3):
        values = everyone[:, f].reshape(total, cols)
        mean = jnp.sum(values, axis=0, keepdims=True) * (1.0 / total)
        center.append(mean)
        devs.append(values - mean)
    dev = jnp.concatenate(devs, 1)
    cross = dot3((st_hi[...], st_lo[...]), halves(dev))
    weights = dispersion * dot3(halves(poly[...]), halves(cross))
    whi, wlo = halves(weights)

    def analyse(places):
        innov = jnp.concatenate(
            [
                jnp.concatenate([noise[cc, yy, xx, zz] - sampled[cc, yy, xx, zz] for yy in range(ny)], 1)
                for zz, xx, cc in places
            ],
            0,
        )
        high, low = halves(innov)
        count = innov.shape[0]
        both = dot(jnp.concatenate([high, low], 0), whi)
        gain = both[:count] + (both[count:] + dot(high, wlo))
        for n, (zz, xx, cc) in enumerate(places):
            at = flat(cc, xx, zz)
            for f in range(3):
                result[at, f] = (
                    center[f]
                    + math.sqrt(widen_dispersion) * (everyone[at, f] - center[f])
                    + gain[n * members : (n + 1) * members, f * cols : (f + 1) * cols]
                )

    back = []
    order = offsets + [(0, 0, 0)]
    batch = nx * nc
    for b in range(0, len(order), batch):
        some = order[b : b + batch]
        analyse([shifted(off) for off in some])
        for n, off in enumerate(some):
            if off == (0, 0, 0):
                continue
            zz, xx, cc = shifted(off)
            copy = remote(result.at[flat(cc, xx, zz)], out_ref.at[me], b_send.at[b + n], b_recv.at[b + n],
                          device(zz, xx, cc, y))
            copy.start()
            back.append(copy)
    out_ref[me] = result[me]
    for copy in back:
        copy.wait()


def with_halo(cells, sides, width):
    for axis, dim in sides:
        count = lax.axis_size(axis)
        head = lax.slice_in_dim(cells, 0, width, axis=dim)
        tail = lax.slice_in_dim(cells, cells.shape[dim] - width, cells.shape[dim], axis=dim)
        cells = jnp.concatenate(
            [
                lax.ppermute(tail, axis, [(i, (i + 1) % count) for i in range(count)]),
                cells,
                lax.ppermute(head, axis, [((i + 1) % count, i) for i in range(count)]),
            ],
            axis=dim,
        )
    return cells


def lax_friedrichs(state):
    depth = state[:, 0]
    east = state[:, 1]
    north = state[:, 2]
    press = 0.5 * gravity * depth * depth
    flux_x = jnp.stack([east, east * east / depth + press, east * north / depth], 1)
    flux_y = jnp.stack([north, east * north / depth, north * north / depth + press], 1)
    inner = state[:, :, 1:-1]
    average = 0.25 * (
        state[:, :, 2:] + state[:, :, :-2] + jnp.roll(inner, 1, 3) + jnp.roll(inner, -1, 3)
    )
    middle = flux_x[:, :, 1:-1]
    return (
        average
        - 0.5 * courant * (jnp.roll(middle, -1, 3) - jnp.roll(middle, 1, 3))
        - 0.5 * courant * (flux_y[:, :, 2:] - flux_y[:, :, :-2])
    )


def product(left, right):
    return jnp.dot(left, right, precision=lax.Precision.HIGHEST, preferred_element_type=jnp.float32)


def plain(
    prior_fields,
    measured_point_location,
    measured_depths,
    inverse_noise_deviation,
    sample_noise_draw,
    sample_line_labels,
):
    dispersion_multiplier = math.sqrt(widen_dispersion / (sample_noise_draw.shape[0] - 1))
    propagated_fields = prior_fields
    for step in range(STEPS):
        padded = with_halo(propagated_fields, (("run", 2),), 1)
        propagated_fields = lax_friedrichs(padded)
    members = propagated_fields.shape[0]
    depth_flat = propagated_fields[:, 0].reshape(
        members, propagated_fields.shape[2] * propagated_fields.shape[3]
    )
    sampled = inverse_noise_deviation[None, :] * jnp.take(
        depth_flat, measured_point_location, axis=1
    )
    innovation = (
        inverse_noise_deviation[None, :] * measured_depths[None, :]
        - sampled
        + jnp.take(sample_noise_draw, sample_line_labels, axis=0)
    )
    all_sampled, all_innov = (
        lax.all_gather(sampled, ("role", "grp"), axis=0, tiled=True),
        lax.all_gather(innovation, ("role", "grp"), axis=0, tiled=True),
    )
    spread = dispersion_multiplier * (all_sampled - jnp.mean(all_sampled, axis=0, keepdims=True))
    first = lax.axis_index(("role", "grp")) * members
    own_spread = lax.dynamic_slice_in_dim(spread, first, members, 0)
    own_innov = lax.dynamic_slice_in_dim(all_innov, first, members, 0)
    gram_rows, cross_rows = (
        lax.psum_scatter(product(own_spread, spread.T), "run", scatter_dimension=0, tiled=True),
        lax.psum_scatter(product(own_innov, spread.T), "run", scatter_dimension=0, tiled=True),
    )
    gram = lax.all_gather(gram_rows, ("role", "grp", "run"), axis=0, tiled=True)
    upper = 1.0 + jnp.sqrt(jnp.sum(gram * gram))
    theta = (upper + 1.0) / 2.0
    delta = (upper - 1.0) / 2.0
    sigma = theta / delta
    rho = 1.0 / sigma
    residual = cross_rows
    direction = residual / theta
    linear_solution = direction
    for turn in range(CHEB - 1):
        residual = residual - direction - product(direction, gram)
        rho_next = 1.0 / (2.0 * sigma - rho)
        direction = rho_next * rho * direction + 2.0 * rho_next / delta * residual
        linear_solution = linear_solution + direction
        rho = rho_next
    posterior_coefficients = lax.all_gather(
        linear_solution, ("role", "grp", "run"), axis=0, tiled=True
    )
    ensemble_combination = (
        math.sqrt(widen_dispersion) * jnp.eye(posterior_coefficients.shape[0], dtype=jnp.float32)
        + dispersion_multiplier * posterior_coefficients
    )
    strip_slab = lax.all_to_all(
        propagated_fields, ("role", "grp"), split_axis=2, concat_axis=0, tiled=True
    )
    array_shape = strip_slab.shape
    flat = strip_slab.reshape(array_shape[0], array_shape[1] * array_shape[2] * array_shape[3])
    center = jnp.mean(flat, axis=0, keepdims=True)
    updated = (center + product(ensemble_combination, flat - center)).reshape(array_shape)
    return lax.all_to_all(updated, ("role", "grp"), split_axis=0, concat_axis=2, tiled=True)


def fused(
    dims,
    prior_fields,
    measured_point_location,
    measured_depths,
    inverse_noise_deviation,
    sample_noise_draw,
    sample_line_labels,
):
    nz, nx, nc, ny = dims
    members, _, rows, cols = prior_fields.shape
    obs = measured_point_location.shape[0]
    every = ny * obs
    group = nz * nx * nc
    slab = (group, 3, members, cols)
    gathered = (nc, ny, nx, nz, members, obs)
    dma = pltpu.SemaphoreType.DMA
    out = pl.pallas_call(
        functools.partial(kernel, dims),
        out_shape=jax.ShapeDtypeStruct(slab, jnp.float32),
        in_specs=[pl.BlockSpec(memory_space=pltpu.SMEM)] + [pl.BlockSpec(memory_space=pltpu.VMEM)] * 5,
        out_specs=pl.BlockSpec(memory_space=pltpu.VMEM),
        scratch_shapes=[
            pltpu.VMEM((2, STEPS, 3, members, cols), jnp.float32),
            pltpu.VMEM(slab, jnp.float32),
            pltpu.VMEM(slab, jnp.float32),
            pltpu.VMEM(slab, jnp.float32),
            pltpu.VMEM(gathered, jnp.float32),
            pltpu.VMEM(gathered, jnp.float32),
            pltpu.VMEM((rows * cols, obs), jnp.bfloat16),
            pltpu.VMEM((every, group * members), jnp.bfloat16),
            pltpu.VMEM((every, group * members), jnp.bfloat16),
            pltpu.VMEM((every, every), jnp.bfloat16),
            pltpu.VMEM((every, every), jnp.bfloat16),
            pltpu.VMEM((every, every), jnp.float32),
            pltpu.VMEM((every, every), jnp.float32),
            pltpu.VMEM((every, every), jnp.float32),
            dma((2 * CHUNKS,)),
            dma((2 * CHUNKS,)),
            dma((CHUNKS * (nz + 6),)),
            dma((CHUNKS * (nz + 6),)),
            dma((nz + 6,)),
            dma((nz + 6,)),
            dma((CHUNKS * group,)),
            dma((CHUNKS * group,)),
            dma((group,)),
            dma((group,)),
        ],
        compiler_params=pltpu.CompilerParams(
            collective_id=0, has_side_effects=True, vmem_limit_bytes=60 * 1024 * 1024
        ),
        name="analysis_kernel",
    )(
        sample_line_labels,
        prior_fields.transpose(2, 1, 0, 3),
        measured_point_location[None, :],
        inverse_noise_deviation[None, :],
        measured_depths[None, :],
        sample_noise_draw,
    )
    return out.transpose(2, 1, 0, 3)


def shards(shape, *args):
    nz, grp, ny = shape["role"], shape["grp"], shape["run"]
    members, _, rows, cols = args[0].shape
    fits = (
        grp == 4
        and ny == 2
        and rows == nz * grp
        and members % (CHUNKS * TILE) == 0
        and cols == 128
        and args[1].shape[0] * ny <= 512
    )
    if fits:
        return fused((nz, 2, 2, ny), *args)
    return plain(*args)


def solution(mesh):
    placed = (
        P(("role", "grp"), None, "run", None),
        P("run"),
        P("run"),
        P("run"),
        P(None, "run"),
        P(("role", "grp")),
    )
    return jax.shard_map(
        functools.partial(shards, dict(mesh.shape)),
        mesh=mesh,
        in_specs=placed,
        out_specs=P(("role", "grp"), None, "run", None),
        check_vma=False,
    )
```

```python
import functools
import math

import jax
import jax.numpy as jnp
from jax import lax
from jax.experimental import pallas as pl
from jax.experimental.pallas import tpu as pltpu
from jax.sharding import PartitionSpec as P

STEPS = 4
CHEB = 8
CHUNKS = 4
TILE = 8

gravity = 1.0
courant = 0.35
widen_dispersion = 1.1

MESH = pl.DeviceIdType.MESH


def advance(fields):
    depth, east, north = fields
    half = 0.5 * courant
    inverse = 1.0 / depth
    press = 0.5 * gravity * depth * depth
    speed_x = east * inverse
    speed_y = north * inverse
    mixed = east * speed_y
    flux_x = (east, east * speed_x + press, mixed)
    flux_y = (north, mixed, north * speed_y + press)
    rows = depth.shape[0]
    out = []
    for q, fx, fy in zip(fields, flux_x, flux_y):
        quarter = 0.25 * q
        mid = quarter[1:-1]
        kx = half * fx[1:-1]
        sides = pltpu.roll(mid - kx, q.shape[2] - 1, 2) + pltpu.roll(mid + kx, 1, 2)
        up = (quarter - half * fy)[2:]
        down = (quarter + half * fy)[: rows - 2]
        out.append(sides + up + down)
    return tuple(out)


def halves(value):
    high = value.astype(jnp.bfloat16)
    return high, (value - high.astype(jnp.float32)).astype(jnp.bfloat16)


def dot(left, right, dims=((1,), (0,))):
    return lax.dot_general(left, right, (dims, ((), ())), preferred_element_type=jnp.float32)


def dot3(left, right, dims=((1,), (0,))):
    (lh, ll), (rh, rl) = left, right
    return dot(lh, rh, dims) + (dot(lh, rl, dims) + dot(ll, rh, dims))


def kernel(
    dims,
    label_ref, x_ref, loc_ref, inv_ref, meas_ref, table_ref,
    out_ref,
    halo, stepped, everyone, result, sampled, noise, hot,
    st_hi, st_lo, gram_hi, gram_lo, res, direc, poly,
    halo_send, halo_recv, s_send, s_recv, n_send, n_recv, f_send, f_recv, b_send, b_recv,
):
    nz, nx, nc, ny = dims
    z = lax.axis_index("role")
    grp = lax.axis_index("grp")
    y = lax.axis_index("run")
    x = grp // nc
    c = grp % nc
    rows, _, members, cols = x_ref.shape
    obs = loc_ref.shape[1]
    total = nz * nx * nc * members
    width = halo.shape[1]

    def device(zz, xx, cc, yy):
        return (zz, xx * nc + cc, yy)

    def flat(cc, xx, zz):
        return (cc * nx + xx) * nz + zz

    me = flat(c, x, z)
    offsets = [(dz, dx, dc) for dz in range(nz) for dx in range(nx) for dc in range(nc)][1:]
    far = {0: 0, nz // 2: 2}
    offsets.sort(key=lambda o: (-far.get(o[0], 1), o[0], -o[1], -o[2]))

    def shifted(off):
        dz, dx, dc = off
        return lax.rem(z + dz, nz), lax.rem(x + dx, nx), lax.rem(c + dc, nc)

    other_y = lax.rem(y + 1, ny)

    barrier = pltpu.get_barrier_semaphore()
    for off in offsets:
        zz, xx, cc = shifted(off)
        pl.semaphore_signal(barrier, inc=1, device_id=device(zz, xx, cc, y), device_id_type=MESH)
    pl.semaphore_signal(barrier, inc=1, device_id=device(z, x, c, other_y), device_id_type=MESH)
    pl.semaphore_wait(barrier, len(offsets) + 1)

    def remote(src, dst, send, recv, target):
        return pltpu.make_async_remote_copy(
            src_ref=src, dst_ref=dst, send_sem=send, recv_sem=recv, device_id=target, device_id_type=MESH
        )

    per = members // CHUNKS
    halo_copies = []
    for k in range(CHUNKS):
        part = pl.ds(k * per, per)
        pair = (
            remote(x_ref.at[pl.ds(rows - width, width), :, part], halo.at[0, :, :, part],
                   halo_send.at[2 * k], halo_recv.at[2 * k], device(z, x, c, other_y)),
            remote(x_ref.at[pl.ds(0, width), :, part], halo.at[1, :, :, part],
                   halo_send.at[2 * k + 1], halo_recv.at[2 * k + 1], device(z, x, c, other_y)),
        )
        for copy in pair:
            copy.start()
        halo_copies.append(pair)

    xo = lax.rem(x + 1, nx)
    co = lax.rem(c + 1, nc)
    east_side = device(z, xo, c, y)
    north_side = device(z, x, c, other_y)
    twin = device(z, x, co, y)
    hops = nz - 1

    class Gather:
        def __init__(self, buf, send, recv, base, part):
            self.buf, self.send, self.recv, self.base, self.part = buf, send, recv, base, part
            self.open = {}

        def go(self, name, slot, line, one, target):
            yy, xx = line
            where = (c, yy, xx, z, self.part) if one else (c, yy, xx, slice(None), self.part)
            piece = self.buf.at[where]
            copy = remote(piece, piece, self.send.at[self.base + slot], self.recv.at[self.base + slot], target)
            copy.start()
            self.open[name] = copy

        def take(self, name):
            self.open.pop(name).wait()

        def first(self):
            for d in range(1, nz):
                self.go(("z", d), d - 1, (y, x), True, device(lax.rem(z + d, nz), x, c, y))

        def spread(self, north=True):
            for d in range(1, nz):
                self.take(("z", d))
            if north:
                self.north()
            self.go("x", hops + 1, (y, x), False, east_side)
            self.go("c0", hops + 3, (y, x), False, twin)

        def north(self):
            self.go("y", hops, (y, x), False, north_side)

        def relay_east(self):
            self.take("x")
            self.go("c1", hops + 4, (y, xo), False, twin)

        def relay_north(self):
            self.take("y")
            self.go("xo", hops + 2, (other_y, x), False, east_side)
            self.go("c2", hops + 5, (other_y, x), False, twin)

        def relay_last(self):
            self.take("xo")
            self.go("c3", hops + 6, (other_y, xo), False, twin)

        def finish(self):
            for name in list(self.open):
                self.take(name)

    def fetch(i, carry):
        noise[c, y, x, z, pl.ds(i, 1)] = table_ref[pl.ds(label_ref[i], 1)]
        return carry

    lax.fori_loop(0, members, fetch, 0)
    noise[c, y, x, z] = noise[c, y, x, z] + inv_ref[...] * meas_ref[...]
    noise_gather = Gather(noise, n_send, n_recv, 0, slice(None))
    noise_gather.first()

    loc = loc_ref[...]
    lanes = lax.broadcasted_iota(jnp.int32, (cols, obs), 0)

    def mark(r, carry):
        at = pl.ds(pl.multiple_of(r * cols, cols), cols)
        hot[at] = jnp.where(loc - r * cols == lanes, 1.0, 0.0).astype(jnp.bfloat16)
        return carry

    lax.fori_loop(0, rows, mark, 0)

    gathers = []
    forward = []
    early = (0, nz // 2)

    def ship(off, part, slot):
        zz, xx, cc = shifted(off)
        copy = remote(stepped.at[flat(cc, xx, zz), :, part], everyone.at[me, :, part],
                      f_send.at[slot], f_recv.at[slot], device(zz, xx, cc, y))
        copy.start()
        forward.append(copy)

    def ship_early(k, part):
        for i, off in enumerate(offsets):
            if off[0] in early:
                ship(off, part, k * len(offsets) + i)

    def ship_late(dx):
        for i, off in enumerate(offsets):
            if off[0] not in early and off[1] == dx:
                ship(off, slice(None), i)
    for k in range(CHUNKS):
        for copy in halo_copies[k]:
            copy.wait()

        def tile(t, carry):
            at = pl.ds(pl.multiple_of(k * per + t * TILE, TILE), TILE)
            fields = tuple(
                jnp.concatenate([halo[0, :, f, at], x_ref[:, f, at], halo[1, :, f, at]], 0) for f in range(3)
            )
            for step in range(STEPS):
                fields = advance(fields)
            for f in range(3):
                stepped[:, f, at] = fields[f]
            return carry

        lax.fori_loop(0, per // TILE, tile, 0)

        part = pl.ds(k * per, per)
        depth = jnp.concatenate([stepped[r, 0, part] for r in range(rows)], 1)
        d1 = depth.astype(jnp.bfloat16)
        rest = depth - d1.astype(jnp.float32)
        d2 = rest.astype(jnp.bfloat16)
        d3 = (rest - d2.astype(jnp.float32)).astype(jnp.bfloat16)
        found = dot(jnp.concatenate([d1, d2, d3], 0), hot[...])
        found = found[:per] + (found[per : 2 * per] + found[2 * per :])
        sampled[c, y, x, z, part] = inv_ref[...] * found
        gather = Gather(sampled, s_send, s_recv, k * (hops + 7), part)
        gather.first()
        gathers.append(gather)
        if k > 0:
            gathers[k - 1].spread()
        else:
            noise_gather.spread(north=False)
        if k < CHUNKS - 1:
            ship_early(k, part)

    gathers[-1].spread()
    ship_early(CHUNKS - 1, pl.ds((CHUNKS - 1) * per, per))
    ship_late(0)
    everyone[me] = stepped[me]
    for gather in gathers:
        gather.relay_north()
    ship_late(1)
    for gather in gathers:
        gather.relay_east()
    noise_gather.north()
    noise_gather.relay_east()
    for gather in gathers:
        gather.relay_last()
    for gather in gathers:
        gather.finish()

    dispersion = math.sqrt(widen_dispersion / (total - 1))
    for yy in range(ny):
        block = sampled[:, yy].reshape(total, obs)
        spread = dispersion * (block - jnp.sum(block, axis=0, keepdims=True) * (1.0 / total))
        hi, lo = halves(spread.T)
        st_hi[pl.ds(yy * obs, obs)] = hi
        st_lo[pl.ds(yy * obs, obs)] = lo

    nt = ((1,), (1,))
    every = ny * obs
    sth = st_hi[...]
    stl = st_lo[...]
    gram = dot3((sth, stl), (sth, stl), nt)
    ghi, glo = halves(gram)
    gram_hi[...] = ghi
    gram_lo[...] = glo
    upper = 1.0 + jnp.sqrt(jnp.sum(jnp.sum(gram * gram, axis=1, keepdims=True), axis=0, keepdims=True))
    theta = (upper + 1.0) / 2.0
    delta = (upper - 1.0) / 2.0
    sigma = theta / delta
    eye = jnp.where(
        lax.broadcasted_iota(jnp.int32, (every, every), 0) == lax.broadcasted_iota(jnp.int32, (every, every), 1),
        1.0, 0.0,
    )
    res[...] = eye
    start = eye * (1.0 / theta)
    direc[...] = start
    poly[...] = start

    noise_gather.relay_north()

    def turn(i, rho):
        d = direc[...]
        prod = dot3(halves(d), (gram_hi[...], gram_lo[...]))
        r = res[...] - d - prod
        res[...] = r
        rho_next = 1.0 / (2.0 * sigma - rho)
        d = (rho_next * rho) * d + (2.0 * rho_next / delta) * r
        direc[...] = d
        poly[...] = poly[...] + d
        return rho_next

    lax.fori_loop(0, CHEB - 1, turn, 1.0 / sigma)

    noise_gather.relay_last()
    for copy in forward:
        copy.wait()
    noise_gather.finish()

    center = []
    devs = []
    for f in range(3):
        values = everyone[:, f].reshape(total, cols)
        mean = jnp.sum(values, axis=0, keepdims=True) * (1.0 / total)
        center.append(mean)
        devs.append(values - mean)
    dev = jnp.concatenate(devs, 1)
    cross = dot3((st_hi[...], st_lo[...]), halves(dev))
    weights = dispersion * dot3(halves(poly[...]), halves(cross))
    whi, wlo = halves(weights)

    def analyse(places):
        innov = jnp.concatenate(
            [
                jnp.concatenate([noise[cc, yy, xx, zz] - sampled[cc, yy, xx, zz] for yy in range(ny)], 1)
                for zz, xx, cc in places
            ],
            0,
        )
        high, low = halves(innov)
        count = innov.shape[0]
        both = dot(jnp.concatenate([high, low], 0), whi)
        gain = both[:count] + (both[count:] + dot(high, wlo))
        for n, (zz, xx, cc) in enumerate(places):
            at = flat(cc, xx, zz)
            for f in range(3):
                result[at, f] = (
                    center[f]
                    + math.sqrt(widen_dispersion) * (everyone[at, f] - center[f])
                    + gain[n * members : (n + 1) * members, f * cols : (f + 1) * cols]
                )

    back = []
    order = offsets + [(0, 0, 0)]
    batch = nx * nc
    for b in range(0, len(order), batch):
        some = order[b : b + batch]
        analyse([shifted(off) for off in some])
        for n, off in enumerate(some):
            if off == (0, 0, 0):
                continue
            zz, xx, cc = shifted(off)
            copy = remote(result.at[flat(cc, xx, zz)], out_ref.at[me], b_send.at[b + n], b_recv.at[b + n],
                          device(zz, xx, cc, y))
            copy.start()
            back.append(copy)
    out_ref[me] = result[me]
    for copy in back:
        copy.wait()


def with_halo(cells, sides, width):
    for axis, dim in sides:
        count = lax.axis_size(axis)
        head = lax.slice_in_dim(cells, 0, width, axis=dim)
        tail = lax.slice_in_dim(cells, cells.shape[dim] - width, cells.shape[dim], axis=dim)
        cells = jnp.concatenate(
            [
                lax.ppermute(tail, axis, [(i, (i + 1) % count) for i in range(count)]),
                cells,
                lax.ppermute(head, axis, [((i + 1) % count, i) for i in range(count)]),
            ],
            axis=dim,
        )
    return cells


def lax_friedrichs(state):
    depth = state[:, 0]
    east = state[:, 1]
    north = state[:, 2]
    press = 0.5 * gravity * depth * depth
    flux_x = jnp.stack([east, east * east / depth + press, east * north / depth], 1)
    flux_y = jnp.stack([north, east * north / depth, north * north / depth + press], 1)
    inner = state[:, :, 1:-1]
    average = 0.25 * (
        state[:, :, 2:] + state[:, :, :-2] + jnp.roll(inner, 1, 3) + jnp.roll(inner, -1, 3)
    )
    middle = flux_x[:, :, 1:-1]
    return (
        average
        - 0.5 * courant * (jnp.roll(middle, -1, 3) - jnp.roll(middle, 1, 3))
        - 0.5 * courant * (flux_y[:, :, 2:] - flux_y[:, :, :-2])
    )


def product(left, right):
    return jnp.dot(left, right, precision=lax.Precision.HIGHEST, preferred_element_type=jnp.float32)


def plain(
    prior_fields,
    measured_point_location,
    measured_depths,
    inverse_noise_deviation,
    sample_noise_draw,
    sample_line_labels,
):
    dispersion_multiplier = math.sqrt(widen_dispersion / (sample_noise_draw.shape[0] - 1))
    propagated_fields = prior_fields
    for step in range(STEPS):
        padded = with_halo(propagated_fields, (("run", 2),), 1)
        propagated_fields = lax_friedrichs(padded)
    members = propagated_fields.shape[0]
    depth_flat = propagated_fields[:, 0].reshape(
        members, propagated_fields.shape[2] * propagated_fields.shape[3]
    )
    sampled = inverse_noise_deviation[None, :] * jnp.take(
        depth_flat, measured_point_location, axis=1
    )
    innovation = (
        inverse_noise_deviation[None, :] * measured_depths[None, :]
        - sampled
        + jnp.take(sample_noise_draw, sample_line_labels, axis=0)
    )
    all_sampled, all_innov = (
        lax.all_gather(sampled, ("role", "grp"), axis=0, tiled=True),
        lax.all_gather(innovation, ("role", "grp"), axis=0, tiled=True),
    )
    spread = dispersion_multiplier * (all_sampled - jnp.mean(all_sampled, axis=0, keepdims=True))
    first = lax.axis_index(("role", "grp")) * members
    own_spread = lax.dynamic_slice_in_dim(spread, first, members, 0)
    own_innov = lax.dynamic_slice_in_dim(all_innov, first, members, 0)
    gram_rows, cross_rows = (
        lax.psum_scatter(product(own_spread, spread.T), "run", scatter_dimension=0, tiled=True),
        lax.psum_scatter(product(own_innov, spread.T), "run", scatter_dimension=0, tiled=True),
    )
    gram = lax.all_gather(gram_rows, ("role", "grp", "run"), axis=0, tiled=True)
    upper = 1.0 + jnp.sqrt(jnp.sum(gram * gram))
    theta = (upper + 1.0) / 2.0
    delta = (upper - 1.0) / 2.0
    sigma = theta / delta
    rho = 1.0 / sigma
    residual = cross_rows
    direction = residual / theta
    linear_solution = direction
    for turn in range(CHEB - 1):
        residual = residual - direction - product(direction, gram)
        rho_next = 1.0 / (2.0 * sigma - rho)
        direction = rho_next * rho * direction + 2.0 * rho_next / delta * residual
        linear_solution = linear_solution + direction
        rho = rho_next
    posterior_coefficients = lax.all_gather(
        linear_solution, ("role", "grp", "run"), axis=0, tiled=True
    )
    ensemble_combination = (
        math.sqrt(widen_dispersion) * jnp.eye(posterior_coefficients.shape[0], dtype=jnp.float32)
        + dispersion_multiplier * posterior_coefficients
    )
    strip_slab = lax.all_to_all(
        propagated_fields, ("role", "grp"), split_axis=2, concat_axis=0, tiled=True
    )
    array_shape = strip_slab.shape
    flat = strip_slab.reshape(array_shape[0], array_shape[1] * array_shape[2] * array_shape[3])
    center = jnp.mean(flat, axis=0, keepdims=True)
    updated = (center + product(ensemble_combination, flat - center)).reshape(array_shape)
    return lax.all_to_all(updated, ("role", "grp"), split_axis=0, concat_axis=2, tiled=True)


def fused(
    dims,
    prior_fields,
    measured_point_location,
    measured_depths,
    inverse_noise_deviation,
    sample_noise_draw,
    sample_line_labels,
):
    nz, nx, nc, ny = dims
    members, _, rows, cols = prior_fields.shape
    obs = measured_point_location.shape[0]
    every = ny * obs
    group = nz * nx * nc
    slab = (group, 3, members, cols)
    gathered = (nc, ny, nx, nz, members, obs)
    dma = pltpu.SemaphoreType.DMA
    out = pl.pallas_call(
        functools.partial(kernel, dims),
        out_shape=jax.ShapeDtypeStruct(slab, jnp.float32),
        in_specs=[pl.BlockSpec(memory_space=pltpu.SMEM)] + [pl.BlockSpec(memory_space=pltpu.VMEM)] * 5,
        out_specs=pl.BlockSpec(memory_space=pltpu.VMEM),
        scratch_shapes=[
            pltpu.VMEM((2, STEPS, 3, members, cols), jnp.float32),
            pltpu.VMEM(slab, jnp.float32),
            pltpu.VMEM(slab, jnp.float32),
            pltpu.VMEM(slab, jnp.float32),
            pltpu.VMEM(gathered, jnp.float32),
            pltpu.VMEM(gathered, jnp.float32),
            pltpu.VMEM((rows * cols, obs), jnp.bfloat16),
            pltpu.VMEM((every, group * members), jnp.bfloat16),
            pltpu.VMEM((every, group * members), jnp.bfloat16),
            pltpu.VMEM((every, every), jnp.bfloat16),
            pltpu.VMEM((every, every), jnp.bfloat16),
            pltpu.VMEM((every, every), jnp.float32),
            pltpu.VMEM((every, every), jnp.float32),
            pltpu.VMEM((every, every), jnp.float32),
            dma((2 * CHUNKS,)),
            dma((2 * CHUNKS,)),
            dma((CHUNKS * (nz + 6),)),
            dma((CHUNKS * (nz + 6),)),
            dma((nz + 6,)),
            dma((nz + 6,)),
            dma((CHUNKS * group,)),
            dma((CHUNKS * group,)),
            dma((group,)),
            dma((group,)),
        ],
        compiler_params=pltpu.CompilerParams(
            collective_id=0, has_side_effects=True, vmem_limit_bytes=60 * 1024 * 1024
        ),
        name="analysis_kernel",
    )(
        sample_line_labels,
        prior_fields.transpose(2, 1, 0, 3),
        measured_point_location[None, :],
        inverse_noise_deviation[None, :],
        measured_depths[None, :],
        sample_noise_draw,
    )
    return out.transpose(2, 1, 0, 3)


def shards(shape, *args):
    nz, grp, ny = shape["role"], shape["grp"], shape["run"]
    members, _, rows, cols = args[0].shape
    fits = (
        grp == 4
        and ny == 2
        and rows == nz * grp
        and members % (CHUNKS * TILE) == 0
        and cols == 128
        and args[1].shape[0] * ny <= 512
    )
    if fits:
        return fused((nz, 2, 2, ny), *args)
    return plain(*args)


def solution(mesh):
    placed = (
        P(("role", "grp"), None, "run", None),
        P("run"),
        P("run"),
        P("run"),
        P(None, "run"),
        P(("role", "grp")),
    )
    return jax.shard_map(
        functools.partial(shards, dict(mesh.shape)),
        mesh=mesh,
        in_specs=placed,
        out_specs=P(("role", "grp"), None, "run", None),
        check_vma=False,
    )
```
